32 devices in a mesh: tm: 2 (over x), band: 16 (over z, y, core).
Axes of the slice: x: 2, y: 2, z: 4, core: 2. Of those that a mesh axis runs over, the one named last changes fastest.
Arguments:
- samples: bfloat16 [512, 256, 2, 512], P('tm', 'band'), may hold values from -6 to 6
- weights: bfloat16 [256, 2, 512, 512], P('band', None, None, 'tm'), may hold values from -0.25 to 0.25
- prototype: float32 [1024], replicated, may hold values from 0.25 to 1
Outputs:
- beam_series: float32 [512, 131072], P('band', 'tm')
The draws below stay inside these ranges and needn't reach their ends.
All inputs are finite; a program needn't handle non-finite values.
Results may differ from the reference program's by a relative error of at most 0.004.
Values may be sent and summed in bfloat16 or wider, within the bound.
A program may use at most 128 MiB of HBM per device.

```python
import math
import jax
import jax.numpy as jnp
from jax import lax

M = 512
K = 256
FIRST_BIN = 32
E = 512
B = 512
L = 1024
NF = 512


def steps_of(own_key, dims, cuts, least, top_value):
    gain = 1.0
    for axis_at, parts in cuts:
        draws = jax.random.uniform(jax.random.fold_in(jax.random.fold_in(own_key, 6), axis_at), (parts,), jnp.float32, least / len(cuts), top_value / len(cuts))
        gain = gain * jnp.repeat(jnp.exp(draws), dims[axis_at] // parts).reshape((-1,) + (1,) * (len(dims) - 1 - axis_at))
    return gain


def gaussian(rng, extent, scale, reach, shards=(), kind=jnp.bfloat16):
    level = steps_of(rng, extent, shards, -0.22, 0.18) if shards else 1.0
    array = jax.random.normal(rng, extent, jnp.float32) * scale * level
    return jnp.minimum(jnp.maximum(array, -reach), reach).astype(kind)


def setup_inputs(seed: int = 0) -> dict:
    key_of = jax.random.split(jax.random.key(seed), 4)
    return {
        "samples": gaussian(key_of[0], (NF, K, 2, E), 1.0, 6.0, ((0, 2), (1, 16))),
        "weights": gaussian(key_of[1], (K, 2, E, B), E ** -0.5, 0.25, ((0, 16), (3, 2))),
        "prototype": jnp.clip(jax.random.uniform(key_of[2], (L,), jnp.float32, 0.25, 1.0), 0.25, 1.0),
    }


def synth_table(prototype):
    length = prototype.shape[0]
    bin_index = jnp.arange(K, dtype=jnp.int32) + FIRST_BIN
    tap_index = jnp.arange(length, dtype=jnp.int32)
    phase_index = bin_index[:, None] * tap_index[None, :] % M
    angles = phase_index.astype(jnp.float32) * (2.0 * math.pi / M)
    scaled = prototype.astype(jnp.float32)[None, :] / math.sqrt(K)
    window_table = jnp.stack([jnp.cos(angles) * scaled, -jnp.sin(angles) * scaled], axis=1)
    return window_table.astype(jnp.bfloat16)

def intersection_add(frames, hop_size):
    pieces = frames.shape[-1] // hop_size
    pieces_view = frames.reshape(frames.shape[:-1] + (pieces, hop_size))
    leading = [(0, 0)] * (pieces_view.ndim - 3)
    intersection = jnp.zeros(pieces_view.shape[:-3] + (pieces_view.shape[-3] + pieces - 1, hop_size), frames.dtype)
    for lag in range(pieces):
        intersection = intersection + jnp.pad(pieces_view[..., lag, :], leading + [(lag, pieces - 1 - lag), (0, 0)])
    return intersection

def reference(samples, weights, prototype):
    hop_size = M // 2
    frame_total = samples.shape[0]

    def form_bin(operands):
        bin_samples, bin_weights = operands
        products = jnp.einsum('fce,deb->bdcf', bin_samples.astype(jnp.float32), bin_weights.astype(jnp.float32), precision=lax.Precision.HIGHEST)
        real_part = products[:, 0, 0] + products[:, 1, 1]
        imag_part = products[:, 0, 1] - products[:, 1, 0]
        return jnp.stack([real_part, imag_part], axis=1).astype(jnp.bfloat16)
    spectra = lax.map(form_bin, (jnp.moveaxis(samples, 1, 0), weights))
    window_table = synth_table(prototype).astype(jnp.float32)

    def synth_beam(beam_spectra):
        frame_out = jnp.einsum('kcf,kcn->fn', beam_spectra.astype(jnp.float32), window_table, precision=lax.Precision.HIGHEST)
        summed = intersection_add(frame_out, hop_size)
        return summed[:frame_total].reshape(frame_total * hop_size)
    return lax.map(synth_beam, jnp.moveaxis(spectra, 1, 0))
```

```python
import math

import jax
import jax.numpy as jnp
from jax import lax
from jax.sharding import PartitionSpec as P

M = 512
K = 256
FIRST_BIN = 32
CHUNKS = 4


def passed_along(block, axis, distance):
    devices = range(lax.axis_size(axis))
    route = [(i - distance, i) for i in devices if i - distance in devices]
    return lax.ppermute(block, axis, route)


def synth_table(prototype):
    length = prototype.shape[0]
    bin_index = jnp.arange(K, dtype=jnp.int32) + FIRST_BIN
    tap_index = jnp.arange(length, dtype=jnp.int32)
    phase_index = bin_index[:, None] * tap_index[None, :] % M
    angles = phase_index.astype(jnp.float32) * (2.0 * math.pi / M)
    scaled = prototype[None, :] / math.sqrt(K)
    window_table = jnp.stack([jnp.cos(angles) * scaled, -jnp.sin(angles) * scaled], axis=1)
    return window_table.astype(jnp.bfloat16)


def beam_form(samples, weights):
    products = jnp.einsum("fkce,kdeb->bkdcf", samples, weights, preferred_element_type=jnp.float32)
    real_part = products[:, :, 0, 0] + products[:, :, 1, 1]
    imag_part = products[:, :, 0, 1] - products[:, :, 1, 0]
    return jnp.stack([real_part, imag_part], axis=2).astype(jnp.bfloat16)


def shards(samples, weights, prototype):
    hop_size = M // 2
    local = weights.shape[0]
    chunks = math.gcd(CHUNKS, local)
    step = local // chunks
    bands = lax.axis_size("band")
    parts = []
    for g in range(chunks):
        lo = g * step
        full = lax.all_gather(weights[lo : lo + step], "tm", axis=3, tiled=True)
        part = beam_form(samples[:, lo : lo + step], full)
        got = lax.all_to_all(part, "band", split_axis=0, concat_axis=1, tiled=True)
        parts.append(got.reshape(got.shape[0], bands, step, 2, got.shape[3]))
    beams, frame_total = parts[0].shape[0], parts[0].shape[4]
    spectra = jnp.concatenate(parts, axis=2).reshape(beams, K * 2, frame_total)
    length = prototype.shape[0]
    lags = length // hop_size
    table = synth_table(prototype).reshape(K * 2, lags, hop_size)
    kernel = table[:, ::-1, :]
    summed = lax.conv_general_dilated(
        spectra, kernel, (1,), [(lags - 1, lags - 1)],
        dimension_numbers=("NCH", "IHO", "NHC"), preferred_element_type=jnp.float32,
    )
    prev_tail = passed_along(summed[:, frame_total:], "tm", 1)
    block_out = summed[:, :frame_total]
    block_out = jnp.concatenate(
        [block_out[:, : lags - 1] + prev_tail, block_out[:, lags - 1 :]], axis=1
    )
    return block_out.reshape(beams, frame_total * hop_size)


def solution(mesh):
    in_specs = (P("tm", "band", None, None), P("band", None, None, "tm"), P())
    out_specs = P("band", "tm")
    return jax.shard_map(shards, mesh=mesh, in_specs=in_specs, out_specs=out_specs, check_vma=False)
```

```python
import functools
import math

import jax
import jax.numpy as jnp
from jax import lax
from jax.experimental import pallas as pl
from jax.experimental.pallas import tpu as pltpu
from jax.sharding import PartitionSpec as P

M = 512
K = 256
FIRST_BIN = 32
GROUP = 4


def passed_along(block, axis, distance):
    devices = range(lax.axis_size(axis))
    route = [(i - distance, i) for i in devices if i - distance in devices]
    return lax.ppermute(block, axis, route)


def synth_table(prototype):
    length = prototype.shape[0]
    bin_index = jnp.arange(K, dtype=jnp.int32) + FIRST_BIN
    tap_index = jnp.arange(length, dtype=jnp.int32)
    phase_index = bin_index[:, None] * tap_index[None, :] % M
    angles = phase_index.astype(jnp.float32) * (2.0 * math.pi / M)
    scaled = prototype[None, :] / math.sqrt(K)
    window_table = jnp.stack([jnp.cos(angles) * scaled, -jnp.sin(angles) * scaled], axis=1)
    return window_table.astype(jnp.bfloat16)


def synth_kernel(*refs):
    *spectra_refs, table_ref, out_ref, tail_ref = refs
    hop = out_ref.shape[2]
    frames = out_ref.shape[1]
    lags = table_ref.shape[1] // hop
    rows = lax.broadcasted_iota(jnp.int32, (frames, hop), 0)
    for b in range(out_ref.shape[0]):
        columns = [r[:, b].reshape(-1, r.shape[3]) for r in spectra_refs]
        x = jnp.concatenate(columns, axis=0)
        y = lax.dot_general(
            x, table_ref[...], (((0,), (0,)), ((), ())), preferred_element_type=jnp.float32
        )
        main = y[:, :hop]
        tail = jnp.zeros((8, hop), jnp.float32)
        for lag in range(1, lags):
            turned = pltpu.roll(y[:, lag * hop : (lag + 1) * hop], lag, 0)
            main = main + jnp.where(rows >= lag, turned, 0.0)
            tail = tail + jnp.where(rows[:8] < lag, turned[:8], 0.0)
        out_ref[b] = main
        tail_ref[b] = tail


def synthesize(spectra, table, hop_size):
    groups, bands, beams, rows, frames = spectra.shape
    per_step = 2 if beams % 2 == 0 else 1
    specs = [
        pl.BlockSpec((None, bands, per_step, rows, frames), lambda i, g=g: (g, 0, i, 0, 0))
        for g in range(groups)
    ]
    flops = 2 * beams * frames * table.shape[0] * table.shape[1]
    return pl.pallas_call(
        synth_kernel,
        grid=(beams // per_step,),
        in_specs=specs + [pl.BlockSpec(table.shape, lambda i: (0, 0))],
        out_specs=[
            pl.BlockSpec((per_step, frames, hop_size), lambda i: (i, 0, 0)),
            pl.BlockSpec((per_step, 8, hop_size), lambda i: (i, 0, 0)),
        ],
        out_shape=[
            jax.ShapeDtypeStruct((beams, frames, hop_size), jnp.float32),
            jax.ShapeDtypeStruct((beams, 8, hop_size), jnp.float32),
        ],
        cost_estimate=pl.CostEstimate(flops=flops, bytes_accessed=20 << 20, transcendentals=0),
        compiler_params=pltpu.CompilerParams(vmem_limit_bytes=40 << 20),
    )(*([spectra] * groups), table)


def exchange_kernel(
    times, bands, samples_hbm, weights_hbm, out_hbm,
    samples, own, others, laid, sendbuf,
    load_sem, x_send, x_recv, b_send, b_recv,
):
    t = lax.axis_index("tm")
    band = lax.axis_index("band")
    groups = out_hbm.shape[0]
    beams = out_hbm.shape[2]
    width = own.shape[3]
    step = own.shape[0] // groups
    fan = width // beams
    tiles = laid.shape[0]

    barrier = pltpu.get_barrier_semaphore()

    @pl.loop(1, bands)
    def _(hop):
        pl.semaphore_signal(barrier, inc=1, device_id={"band": lax.rem(band + hop, bands)})

    for turn in range(1, times):
        pl.semaphore_signal(barrier, inc=1, device_id={"tm": lax.rem(t + turn, times)})
    pl.semaphore_wait(barrier, bands + times - 2)

    def weights_copy(g, turn):
        part = pl.ds(g * step, step)
        return pltpu.make_async_remote_copy(
            src_ref=weights_hbm.at[part],
            dst_ref=others.at[turn - 1, part],
            send_sem=x_send.at[turn - 1, g],
            recv_sem=x_recv.at[turn - 1, g],
            device_id={"tm": lax.rem(t + turn, times)},
        )

    def loads(g):
        part = pl.ds(g * step, step)
        return (
            pltpu.make_async_copy(samples_hbm.at[part], samples.at[part], load_sem.at[0, g]),
            pltpu.make_async_copy(weights_hbm.at[part], own.at[part], load_sem.at[1, g]),
        )

    for g in range(groups):
        for turn in range(1, times):
            weights_copy(g, turn).start()
    for g in range(groups):
        for copy in loads(g):
            copy.start()

    def spectra_copy(g, turn, i):
        first = lax.rem(t - turn + times, times) * fan
        return pltpu.make_async_remote_copy(
            src_ref=sendbuf.at[g, turn, pl.ds(i * beams, beams)],
            dst_ref=out_hbm.at[g, band],
            send_sem=b_send.at[g, turn, i],
            recv_sem=b_recv.at[g, band],
            device_id={"band": first + i},
        ), pltpu.make_async_copy(
            sendbuf.at[g, turn, pl.ds(i * beams, beams)],
            out_hbm.at[g, band],
            b_recv.at[g, band],
        ), first + i

    def contract(w, s):
        return lax.dot_general(
            w, s, (((0,), (1,)), ((), ())), preferred_element_type=jnp.float32
        )

    def form(g, turn):
        source = own if turn == 0 else others.at[turn - 1]

        @pl.loop(0, step)
        def _(kk):
            k = g * step + kk
            w0, w1 = source[k, 0], source[k, 1]
            s0, s1 = samples[k, 0], samples[k, 1]
            real_part = contract(w0, s0) + contract(w1, s1)
            imag_part = contract(w0, s1) - contract(w1, s0)
            for c, value in enumerate((real_part, imag_part)):
                for f in range(tiles):
                    laid[f, pl.ds(2 * kk + c, width, 2 * step), :] = value[:, f * 128 : (f + 1) * 128]

        for f in range(tiles):
            @pl.loop(0, fan)
            def _(i):
                rows = laid[f, pl.ds(i * beams * 2 * step, beams * 2 * step), :]
                sendbuf[g, turn, pl.ds(i * beams, beams), :, f * 128 : (f + 1) * 128] = (
                    rows.astype(jnp.bfloat16).reshape(beams, 2 * step, 128)
                )

        @pl.loop(0, fan)
        def _(i):
            remote, local, target = spectra_copy(g, turn, i)

            @pl.when(target == band)
            def _():
                local.start()

            @pl.when(target != band)
            def _():
                remote.start()

    @pl.loop(0, groups)
    def _(g):
        for copy in loads(g):
            copy.wait()
        form(g, 0)
        for turn in range(1, times):
            weights_copy(g, turn).wait_recv()
            form(g, turn)

    @pl.loop(0, groups)
    def _(g):
        for turn in range(1, times):
            weights_copy(g, turn).wait_send()
        for turn in range(times):
            @pl.loop(0, fan)
            def _(i):
                remote, _, target = spectra_copy(g, turn, i)

                @pl.when(target != band)
                def _():
                    remote.wait_send()

        @pl.loop(0, bands)
        def _(peer):
            pltpu.make_async_copy(
                out_hbm.at[g, peer], out_hbm.at[g, peer], b_recv.at[g, peer]
            ).wait()


def exchanged_spectra(samples, weights):
    times, bands = lax.axis_size("tm"), lax.axis_size("band")
    local, _, elements, width = weights.shape
    frames = samples.shape[2]
    step = math.gcd(GROUP, local)
    groups = local // step
    beams = width * times // bands
    tiles = frames // 128
    fan = width // beams
    flops = 8 * local * frames * elements * width * times
    return pl.pallas_call(
        functools.partial(exchange_kernel, times, bands),
        in_specs=[pl.BlockSpec(memory_space=pl.ANY)] * 2,
        out_specs=pl.BlockSpec(memory_space=pl.ANY),
        out_shape=jax.ShapeDtypeStruct((groups, bands, beams, 2 * step, frames), jnp.bfloat16),
        scratch_shapes=[
            pltpu.VMEM(samples.shape, jnp.bfloat16),
            pltpu.VMEM(weights.shape, jnp.bfloat16),
            pltpu.VMEM((times - 1,) + weights.shape, jnp.bfloat16),
            pltpu.VMEM((tiles, width * 2 * step, 128), jnp.float32),
            pltpu.VMEM((groups, times, width, 2 * step, frames), jnp.bfloat16),
            pltpu.SemaphoreType.DMA((2, groups)),
            pltpu.SemaphoreType.DMA((times - 1, groups)),
            pltpu.SemaphoreType.DMA((times - 1, groups)),
            pltpu.SemaphoreType.DMA((groups, times, fan)),
            pltpu.SemaphoreType.DMA((groups, bands)),
        ],
        cost_estimate=pl.CostEstimate(flops=flops, bytes_accessed=32 << 20, transcendentals=0),
        compiler_params=pltpu.CompilerParams(
            collective_id=0, has_side_effects=True, vmem_limit_bytes=56 << 20
        ),
    )(samples, weights)


def shards(samples, weights, prototype):
    hop_size = M // 2
    spectra = exchanged_spectra(samples.transpose(1, 2, 0, 3), weights)
    groups, bands, beams, rows, frame_total = spectra.shape
    length = prototype.shape[0]
    table = synth_table(prototype).reshape(bands, groups, rows, length)
    table = table.transpose(1, 0, 2, 3).reshape(K * 2, length)
    main, tail = synthesize(spectra, table, hop_size)
    prev_tail = passed_along(tail, "tm", 1)
    pad = jnp.pad(prev_tail, ((0, 0), (0, frame_total - 8), (0, 0)))
    return (main + pad).reshape(beams, frame_total * hop_size)


def solution(mesh):
    in_specs = (P("tm", "band", None, None), P("band", None, None, "tm"), P())
    out_specs = P("band", "tm")
    return jax.shard_map(shards, mesh=mesh, in_specs=in_specs, out_specs=out_specs, check_vma=False)
```

```python
import functools
import math

import jax
import jax.numpy as jnp
from jax import lax
from jax.experimental import pallas as pl
from jax.experimental.pallas import tpu as pltpu
from jax.sharding import PartitionSpec as P

M = 512
K = 256
FIRST_BIN = 32
GROUP = 1
LANES = 128
SUBLANES = 8


def passed_along(block, axis, distance):
    devices = range(lax.axis_size(axis))
    route = [(i - distance, i) for i in devices if i - distance in devices]
    return lax.ppermute(block, axis, route)


def synth_kernel(*refs):
    *spectra_refs, table_ref, out_ref, tail_ref = refs
    hop = tail_ref.shape[2]
    frames = spectra_refs[0].shape[3]
    lags = table_ref.shape[1] // hop
    pieces = hop // LANES
    per_step = tail_ref.shape[0]
    rows = lax.broadcasted_iota(jnp.int32, (frames, hop), 0)
    for b in range(per_step):
        columns = [r[:, b].reshape(-1, r.shape[3]) for r in spectra_refs]
        x = jnp.concatenate(columns, axis=0)
        y = lax.dot_general(
            x, table_ref[...], (((0,), (0,)), ((), ())), preferred_element_type=jnp.float32
        )
        main = y[:, :hop]
        tail = jnp.zeros((8, hop), jnp.float32)
        for lag in range(1, lags):
            turned = pltpu.roll(y[:, lag * hop : (lag + 1) * hop], lag, 0)
            main = main + jnp.where(rows >= lag, turned, 0.0)
            tail = tail + jnp.where(rows[:8] < lag, turned[:8], 0.0)
        slot = pl.program_id(1) * per_step + b
        for m in range(pieces):
            out_ref[pl.ds(m * SUBLANES + slot, frames, pieces * SUBLANES), :] = (
                main[:, m * LANES : (m + 1) * LANES]
            )
        tail_ref[b] = tail


def synthesize(spectra, table, hop_size):
    groups, bands, beams, rows, frames = spectra.shape
    per_step = 2
    inner = SUBLANES // per_step
    tile_rows = frames * hop_size // LANES * SUBLANES
    specs = [
        pl.BlockSpec(
            (None, bands, per_step, rows, frames), lambda i, j, g=g: (g, 0, i * inner + j, 0, 0)
        )
        for g in range(groups)
    ]
    flops = 2 * beams * frames * table.shape[0] * table.shape[1]
    return pl.pallas_call(
        synth_kernel,
        grid=(beams // SUBLANES, inner),
        in_specs=specs + [pl.BlockSpec(table.shape, lambda i, j: (0, 0))],
        out_specs=[
            pl.BlockSpec((tile_rows, LANES), lambda i, j: (i, 0)),
            pl.BlockSpec((per_step, 8, hop_size), lambda i, j: (i * inner + j, 0, 0)),
        ],
        out_shape=[
            jax.ShapeDtypeStruct((beams // SUBLANES * tile_rows, LANES), jnp.float32),
            jax.ShapeDtypeStruct((beams, 8, hop_size), jnp.float32),
        ],
        cost_estimate=pl.CostEstimate(flops=flops, bytes_accessed=20 << 20, transcendentals=0),
        compiler_params=pltpu.CompilerParams(vmem_limit_bytes=60 << 20),
    )(*([spectra] * groups), table)


def exchange_kernel(
    times, bands, samples_hbm, weights_hbm, prototype_ref, out_hbm, table_ref,
    raw, wide, samples, own, others, laid, sendbuf,
    load_sem, x_send, x_recv, b_send, b_recv,
):
    t = lax.axis_index("tm")
    band = lax.axis_index("band")
    groups = out_hbm.shape[0]
    beams = out_hbm.shape[2]
    width = own.shape[3]
    step = own.shape[0] // groups
    fan = width // beams
    tiles = laid.shape[0]

    barrier = pltpu.get_barrier_semaphore()

    @pl.loop(1, bands)
    def _(hop):
        pl.semaphore_signal(barrier, inc=1, device_id={"band": lax.rem(band + hop, bands)})

    for turn in range(1, times):
        pl.semaphore_signal(barrier, inc=1, device_id={"tm": lax.rem(t + turn, times)})
    pl.semaphore_wait(barrier, bands + times - 2)

    def weights_copy(g, turn):
        part = pl.ds(g * step, step)
        return pltpu.make_async_remote_copy(
            src_ref=weights_hbm.at[part],
            dst_ref=others.at[turn - 1, part],
            send_sem=x_send.at[turn - 1, g],
            recv_sem=x_recv.at[turn - 1, g],
            device_id={"tm": lax.rem(t + turn, times)},
        )

    def loads(g):
        part = pl.ds(g * step, step)
        return (
            pltpu.make_async_copy(samples_hbm.at[:, part], raw.at[:, part], load_sem.at[0, g]),
            pltpu.make_async_copy(weights_hbm.at[part], own.at[part], load_sem.at[1, g]),
        )

    for g in range(groups):
        for turn in range(1, times):
            weights_copy(g, turn).start()
    for g in range(groups):
        for copy in loads(g):
            copy.start()

    def spectra_copy(g, turn, i):
        first = lax.rem(t - turn + times, times) * fan
        return pltpu.make_async_remote_copy(
            src_ref=sendbuf.at[g, turn, pl.ds(i * beams, beams)],
            dst_ref=out_hbm.at[g, band],
            send_sem=b_send.at[g, turn, i],
            recv_sem=b_recv.at[g, band],
            device_id={"band": first + i},
        ), pltpu.make_async_copy(
            sendbuf.at[g, turn, pl.ds(i * beams, beams)],
            out_hbm.at[g, band],
            b_recv.at[g, band],
        ), first + i

    def contract(w, s):
        return lax.dot_general(
            w, s, (((0,), (1,)), ((), ())), preferred_element_type=jnp.float32
        )

    def form(g, turn):
        source = own if turn == 0 else others.at[turn - 1]

        @pl.loop(0, step)
        def _(kk):
            k = g * step + kk
            w0, w1 = source[k, 0], source[k, 1]
            s0, s1 = samples[kk, 0], samples[kk, 1]
            real_part = contract(w0, s0) + contract(w1, s1)
            imag_part = contract(w0, s1) - contract(w1, s0)
            for c, value in enumerate((real_part, imag_part)):
                for f in range(tiles):
                    laid[f, pl.ds(2 * kk + c, width, 2 * step), :] = value[:, f * LANES : (f + 1) * LANES]

        for f in range(tiles):
            @pl.loop(0, fan)
            def _(i):
                rows = laid[f, pl.ds(i * beams * 2 * step, beams * 2 * step), :]
                sendbuf[g, turn, pl.ds(i * beams, beams), :, f * LANES : (f + 1) * LANES] = (
                    rows.astype(jnp.bfloat16).reshape(beams, 2 * step, LANES)
                )

        @pl.loop(0, fan)
        def _(i):
            remote, local, target = spectra_copy(g, turn, i)

            @pl.when(target == band)
            def _():
                local.start()

            @pl.when(target != band)
            def _():
                remote.start()

    frames = raw.shape[0]
    packed = raw.shape[2]

    def separate(g):
        @pl.loop(0, step)
        def _(kk):
            wide[...] = raw[:, g * step + kk].astype(jnp.float32).reshape(frames * packed, LANES)
            for piece in range(packed // 2):
                for c in range(2):
                    plane = wide[pl.ds(2 * piece + c, frames, packed), :]
                    samples[kk, c, :, piece * LANES : (piece + 1) * LANES] = plane.astype(jnp.bfloat16)

    def tabulate(g):
        rows = table_ref.shape[0] // groups
        length = table_ref.shape[1]
        row = lax.broadcasted_iota(jnp.int32, (rows, length), 0)
        tap = lax.broadcasted_iota(jnp.int32, (rows, length), 1)
        part = row // 2
        subband = (part // step) * (step * groups) + g * step + lax.rem(part, step) + FIRST_BIN
        phase = lax.rem(subband * tap + lax.rem(row, 2) * (M // 4), M)
        scaled = jnp.cos(phase.astype(jnp.float32) * (2.0 * math.pi / M)) * (
            prototype_ref[...] / math.sqrt(K)
        )
        table_ref[pl.ds(pl.multiple_of(g * rows, rows), rows), :] = scaled.astype(jnp.bfloat16)

    @pl.loop(0, groups)
    def _(g):
        for copy in loads(g):
            copy.wait()
        separate(g)
        form(g, 0)
        tabulate(g)
        for turn in range(1, times):
            weights_copy(g, turn).wait_recv()
            form(g, turn)

    @pl.loop(0, groups)
    def _(g):
        for turn in range(1, times):
            weights_copy(g, turn).wait_send()
        for turn in range(times):
            @pl.loop(0, fan)
            def _(i):
                remote, _, target = spectra_copy(g, turn, i)

                @pl.when(target != band)
                def _():
                    remote.wait_send()

        @pl.loop(0, bands)
        def _(peer):
            pltpu.make_async_copy(
                out_hbm.at[g, peer], out_hbm.at[g, peer], b_recv.at[g, peer]
            ).wait()


def exchanged_spectra(samples, weights, prototype):
    times, bands = lax.axis_size("tm"), lax.axis_size("band")
    local, _, elements, width = weights.shape
    frames, _, packed, _ = samples.shape
    step = math.gcd(GROUP, local)
    groups = local // step
    beams = width * times // bands
    tiles = frames // LANES
    fan = width // beams
    flops = 8 * local * frames * elements * width * times
    return pl.pallas_call(
        functools.partial(exchange_kernel, times, bands),
        in_specs=[pl.BlockSpec(memory_space=pl.ANY)] * 2 + [pl.BlockSpec(memory_space=pltpu.VMEM)],
        out_specs=[pl.BlockSpec(memory_space=pl.ANY), pl.BlockSpec(memory_space=pltpu.VMEM)],
        out_shape=[
            jax.ShapeDtypeStruct((groups, bands, beams, 2 * step, frames), jnp.bfloat16),
            jax.ShapeDtypeStruct((2 * local * bands, prototype.shape[1]), jnp.bfloat16),
        ],
        scratch_shapes=[
            pltpu.VMEM(samples.shape, jnp.bfloat16),
            pltpu.VMEM((frames * packed, LANES), jnp.float32),
            pltpu.VMEM((step, 2, frames, elements), jnp.bfloat16),
            pltpu.VMEM(weights.shape, jnp.bfloat16),
            pltpu.VMEM((times - 1,) + weights.shape, jnp.bfloat16),
            pltpu.VMEM((tiles, width * 2 * step, LANES), jnp.float32),
            pltpu.VMEM((groups, times, width, 2 * step, frames), jnp.bfloat16),
            pltpu.SemaphoreType.DMA((2, groups)),
            pltpu.SemaphoreType.DMA((times - 1, groups)),
            pltpu.SemaphoreType.DMA((times - 1, groups)),
            pltpu.SemaphoreType.DMA((groups, times, fan)),
            pltpu.SemaphoreType.DMA((groups, bands)),
        ],
        cost_estimate=pl.CostEstimate(flops=flops, bytes_accessed=32 << 20, transcendentals=0),
        compiler_params=pltpu.CompilerParams(
            collective_id=0, has_side_effects=True, vmem_limit_bytes=56 << 20
        ),
    )(samples, weights, prototype)


def shards(samples, weights, prototype):
    hop_size = M // 2
    frames, local, _, elements = samples.shape
    pieces = elements // LANES
    packed = samples.reshape(frames, local, 2, pieces, LANES).transpose(0, 1, 3, 2, 4)
    packed = packed.reshape(frames, local, 2 * pieces, LANES)
    spectra, table = exchanged_spectra(packed, weights, prototype[None, :])
    beams = spectra.shape[2]
    tiles, tail = synthesize(spectra, table, hop_size)
    prev_tail = passed_along(tail, "tm", 1).reshape(beams, -1)
    series = tiles.reshape(beams // SUBLANES, frames * hop_size // LANES, SUBLANES, LANES)
    series = series.transpose(0, 2, 1, 3).reshape(beams, frames * hop_size)
    head = series[:, : prev_tail.shape[1]] + prev_tail
    return lax.dynamic_update_slice(series, head, (0, 0))


def solution(mesh):
    in_specs = (P("tm", "band", None, None), P("band", None, None, "tm"), P())
    out_specs = P("band", "tm")
    return jax.shard_map(shards, mesh=mesh, in_specs=in_specs, out_specs=out_specs, check_vma=False)
```

```python
import functools
import math

import jax
import jax.numpy as jnp
from jax import lax
from jax.experimental import pallas as pl
from jax.experimental.pallas import tpu as pltpu
from jax.sharding import PartitionSpec as P

M = 512
K = 256
FIRST_BIN = 32
GROUP = 1
LANES = 128
SUBLANES = 8


def passed_along(block, axis, distance):
    devices = range(lax.axis_size(axis))
    route = [(i - distance, i) for i in devices if i - distance in devices]
    return lax.ppermute(block, axis, route)


def synth_kernel(*refs):
    *spectra_refs, table_ref, out_ref, tail_ref = refs
    hop = tail_ref.shape[2]
    frames = spectra_refs[0].shape[3]
    lags = table_ref.shape[1] // hop
    pieces = hop // LANES
    per_step = tail_ref.shape[0]
    rows = lax.broadcasted_iota(jnp.int32, (frames, hop), 0)
    for b in range(per_step):
        columns = [r[:, b].reshape(-1, r.shape[3]) for r in spectra_refs]
        x = jnp.concatenate(columns, axis=0)
        y = lax.dot_general(
            x, table_ref[...], (((0,), (0,)), ((), ())), preferred_element_type=jnp.float32
        )
        main = y[:, :hop]
        tail = jnp.zeros((8, hop), jnp.float32)
        for lag in range(1, lags):
            turned = pltpu.roll(y[:, lag * hop : (lag + 1) * hop], lag, 0)
            main = main + jnp.where(rows >= lag, turned, 0.0)
            tail = tail + jnp.where(rows[:8] < lag, turned[:8], 0.0)
        slot = pl.program_id(1) * per_step + b
        for m in range(pieces):
            out_ref[pl.ds(m * SUBLANES + slot, frames, pieces * SUBLANES), :] = (
                main[:, m * LANES : (m + 1) * LANES]
            )
        tail_ref[b] = tail


def synthesize(spectra, table, hop_size):
    groups, bands, beams, rows, frames = spectra.shape
    per_step = 8
    inner = SUBLANES // per_step
    tile_rows = frames * hop_size // LANES * SUBLANES
    specs = [
        pl.BlockSpec(
            (None, bands, per_step, rows, frames), lambda i, j, g=g: (g, 0, i * inner + j, 0, 0)
        )
        for g in range(groups)
    ]
    flops = 2 * beams * frames * table.shape[0] * table.shape[1]
    return pl.pallas_call(
        synth_kernel,
        grid=(beams // SUBLANES, inner),
        in_specs=specs + [pl.BlockSpec(table.shape, lambda i, j: (0, 0))],
        out_specs=[
            pl.BlockSpec((tile_rows, LANES), lambda i, j: (i, 0)),
            pl.BlockSpec((per_step, 8, hop_size), lambda i, j: (i * inner + j, 0, 0)),
        ],
        out_shape=[
            jax.ShapeDtypeStruct((beams // SUBLANES * tile_rows, LANES), jnp.float32),
            jax.ShapeDtypeStruct((beams, 8, hop_size), jnp.float32),
        ],
        cost_estimate=pl.CostEstimate(flops=flops, bytes_accessed=20 << 20, transcendentals=0),
        compiler_params=pltpu.CompilerParams(vmem_limit_bytes=60 << 20),
    )(*([spectra] * groups), table)


def exchange_kernel(
    times, bands, samples_hbm, weights_hbm, prototype_ref, out_hbm, table_ref,
    raw, wide, samples, own, others, laid, sendbuf,
    load_sem, x_send, x_recv, b_send, b_recv,
):
    t = lax.axis_index("tm")
    band = lax.axis_index("band")
    groups = out_hbm.shape[0]
    beams = out_hbm.shape[2]
    width = own.shape[3]
    step = own.shape[0] // groups
    fan = width // beams
    tiles = laid.shape[0]

    barrier = pltpu.get_barrier_semaphore()

    @pl.loop(1, bands)
    def _(hop):
        pl.semaphore_signal(barrier, inc=1, device_id={"band": lax.rem(band + hop, bands)})

    for turn in range(1, times):
        pl.semaphore_signal(barrier, inc=1, device_id={"tm": lax.rem(t + turn, times)})
    pl.semaphore_wait(barrier, bands + times - 2)

    def weights_copy(g, turn):
        part = pl.ds(g * step, step)
        return pltpu.make_async_remote_copy(
            src_ref=weights_hbm.at[part],
            dst_ref=others.at[turn - 1, part],
            send_sem=x_send.at[turn - 1, g],
            recv_sem=x_recv.at[turn - 1, g],
            device_id={"tm": lax.rem(t + turn, times)},
        )

    def loads(g):
        part = pl.ds(g * step, step)
        return (
            pltpu.make_async_copy(samples_hbm.at[:, part], raw.at[:, part], load_sem.at[0, g]),
            pltpu.make_async_copy(weights_hbm.at[part], own.at[part], load_sem.at[1, g]),
        )

    for g in range(groups):
        for turn in range(1, times):
            weights_copy(g, turn).start()
    for g in range(groups):
        for copy in loads(g):
            copy.start()

    def spectra_copy(g, turn, i):
        first = lax.rem(t - turn + times, times) * fan
        return pltpu.make_async_remote_copy(
            src_ref=sendbuf.at[g, turn, pl.ds(i * beams, beams)],
            dst_ref=out_hbm.at[g, band],
            send_sem=b_send.at[g, turn, i],
            recv_sem=b_recv.at[g, band],
            device_id={"band": first + i},
        ), pltpu.make_async_copy(
            sendbuf.at[g, turn, pl.ds(i * beams, beams)],
            out_hbm.at[g, band],
            b_recv.at[g, band],
        ), first + i

    def contract(w, s):
        return lax.dot_general(
            w, s, (((0,), (1,)), ((), ())), preferred_element_type=jnp.float32
        )

    def form(g, turn):
        source = own if turn == 0 else others.at[turn - 1]

        @pl.loop(0, step)
        def _(kk):
            k = g * step + kk
            w0, w1 = source[k, 0], source[k, 1]
            s0, s1 = samples[kk, 0], samples[kk, 1]
            real_part = contract(w0, s0) + contract(w1, s1)
            imag_part = contract(w0, s1) - contract(w1, s0)
            for c, value in enumerate((real_part, imag_part)):
                for f in range(tiles):
                    laid[f, pl.ds(2 * kk + c, width, 2 * step), :] = value[:, f * LANES : (f + 1) * LANES]

        for f in range(tiles):
            @pl.loop(0, fan)
            def _(i):
                rows = laid[f, pl.ds(i * beams * 2 * step, beams * 2 * step), :]
                sendbuf[g, turn, pl.ds(i * beams, beams), :, f * LANES : (f + 1) * LANES] = (
                    rows.astype(jnp.bfloat16).reshape(beams, 2 * step, LANES)
                )

        @pl.loop(0, fan)
        def _(i):
            remote, local, target = spectra_copy(g, turn, i)

            @pl.when(target == band)
            def _():
                local.start()

            @pl.when(target != band)
            def _():
                remote.start()

    frames = raw.shape[0]
    packed = raw.shape[2]

    def separate(g):
        @pl.loop(0, step)
        def _(kk):
            wide[...] = raw[:, g * step + kk].astype(jnp.float32).reshape(frames * packed, LANES)
            for piece in range(packed // 2):
                for c in range(2):
                    plane = wide[pl.ds(2 * piece + c, frames, packed), :]
                    samples[kk, c, :, piece * LANES : (piece + 1) * LANES] = plane.astype(jnp.bfloat16)

    def tabulate(g):
        rows = table_ref.shape[0] // groups
        length = table_ref.shape[1]
        row = lax.broadcasted_iota(jnp.int32, (rows, length), 0)
        tap = lax.broadcasted_iota(jnp.int32, (rows, length), 1)
        part = row // 2
        subband = (part // step) * (step * groups) + g * step + lax.rem(part, step) + FIRST_BIN
        phase = lax.rem(subband * tap + lax.rem(row, 2) * (M // 4), M)
        scaled = jnp.cos(phase.astype(jnp.float32) * (2.0 * math.pi / M)) * (
            prototype_ref[...] / math.sqrt(K)
        )
        table_ref[pl.ds(pl.multiple_of(g * rows, rows), rows), :] = scaled.astype(jnp.bfloat16)

    @pl.loop(0, groups)
    def _(g):
        for copy in loads(g):
            copy.wait()
        separate(g)
        form(g, 0)
        tabulate(g)
        for turn in range(1, times):
            weights_copy(g, turn).wait_recv()
            form(g, turn)

    @pl.loop(0, groups)
    def _(g):
        for turn in range(1, times):
            weights_copy(g, turn).wait_send()
        for turn in range(times):
            @pl.loop(0, fan)
            def _(i):
                remote, _, target = spectra_copy(g, turn, i)

                @pl.when(target != band)
                def _():
                    remote.wait_send()

        @pl.loop(0, bands)
        def _(peer):
            pltpu.make_async_copy(
                out_hbm.at[g, peer], out_hbm.at[g, peer], b_recv.at[g, peer]
            ).wait()


def exchanged_spectra(samples, weights, prototype):
    times, bands = lax.axis_size("tm"), lax.axis_size("band")
    local, _, elements, width = weights.shape
    frames, _, packed, _ = samples.shape
    step = math.gcd(GROUP, local)
    groups = local // step
    beams = width * times // bands
    tiles = frames // LANES
    fan = width // beams
    flops = 8 * local * frames * elements * width * times
    return pl.pallas_call(
        functools.partial(exchange_kernel, times, bands),
        in_specs=[pl.BlockSpec(memory_space=pl.ANY)] * 2 + [pl.BlockSpec(memory_space=pltpu.VMEM)],
        out_specs=[pl.BlockSpec(memory_space=pl.ANY), pl.BlockSpec(memory_space=pltpu.VMEM)],
        out_shape=[
            jax.ShapeDtypeStruct((groups, bands, beams, 2 * step, frames), jnp.bfloat16),
            jax.ShapeDtypeStruct((2 * local * bands, prototype.shape[1]), jnp.bfloat16),
        ],
        scratch_shapes=[
            pltpu.VMEM(samples.shape, jnp.bfloat16),
            pltpu.VMEM((frames * packed, LANES), jnp.float32),
            pltpu.VMEM((step, 2, frames, elements), jnp.bfloat16),
            pltpu.VMEM(weights.shape, jnp.bfloat16),
            pltpu.VMEM((times - 1,) + weights.shape, jnp.bfloat16),
            pltpu.VMEM((tiles, width * 2 * step, LANES), jnp.float32),
            pltpu.VMEM((groups, times, width, 2 * step, frames), jnp.bfloat16),
            pltpu.SemaphoreType.DMA((2, groups)),
            pltpu.SemaphoreType.DMA((times - 1, groups)),
            pltpu.SemaphoreType.DMA((times - 1, groups)),
            pltpu.SemaphoreType.DMA((groups, times, fan)),
            pltpu.SemaphoreType.DMA((groups, bands)),
        ],
        cost_estimate=pl.CostEstimate(flops=flops, bytes_accessed=32 << 20, transcendentals=0),
        compiler_params=pltpu.CompilerParams(
            collective_id=0, has_side_effects=True, vmem_limit_bytes=56 << 20
        ),
    )(samples, weights, prototype)


def shards(samples, weights, prototype):
    hop_size = M // 2
    frames, local, _, elements = samples.shape
    pieces = elements // LANES
    packed = samples.reshape(frames, local, 2, pieces, LANES).transpose(0, 1, 3, 2, 4)
    packed = packed.reshape(frames, local, 2 * pieces, LANES)
    spectra, table = exchanged_spectra(packed, weights, prototype[None, :])
    beams = spectra.shape[2]
    tiles, tail = synthesize(spectra, table, hop_size)
    prev_tail = passed_along(tail, "tm", 1).reshape(beams, -1)
    series = tiles.reshape(beams // SUBLANES, frames * hop_size // LANES, SUBLANES, LANES)
    series = series.transpose(0, 2, 1, 3).reshape(beams, frames * hop_size)
    head = series[:, : prev_tail.shape[1]] + prev_tail
    return lax.dynamic_update_slice(series, head, (0, 0))


def solution(mesh):
    in_specs = (P("tm", "band", None, None), P("band", None, None, "tm"), P())
    out_specs = P("band", "tm")
    return jax.shard_map(shards, mesh=mesh, in_specs=in_specs, out_specs=out_specs, check_vma=False)
```
